32 devices in a mesh: ens: 2 (over y), tm: 4 (over x, core), space: 4 (over z).
Axes of the slice: x: 2, y: 2, z: 4, core: 2. Of those that a mesh axis runs over, the one named last changes fastest.
Arguments:
- eigvecs: bfloat16 [8, 2, 3, 2048, 256], P(('ens', 'tm'), None, None, 'space'), parts along dimension 0, may hold values from -6 to 6
- links: bfloat16 [8, 3, 2, 3, 3, 2048], P(('ens', 'tm'), None, None, None, None, 'space'), parts along dimension 0, may hold values from -2.5 to 2.5
- momenta: int32 [3, 3], replicated, may hold values from -2 to 2
- perambulators: bfloat16 [8, 2, 256, 256], P(('ens', 'tm')), parts along dimension 0, may hold values from -0.25 to 0.25
Outputs:
- elementals: bfloat16 [8, 256, 3, 2, 256], P(('ens', 'tm'), 'space'), parts along dimension 0
- projected: bfloat16 [8, 4, 256, 3, 2, 256], P(('ens', 'tm'), None, 'space'), parts along dimension 0
The draws below stay inside these ranges and needn't reach their ends.
There are 2 independent parts, one for each index of `ens`. The reference program is written for one: setup_inputs(seed, part) draws one part's arguments, and reference() takes and returns one part's arrays. A program takes and returns all parts, laid end to end along the dimension named above; an argument that names none is the same for every part. Nothing has to cross between parts.
All inputs are finite; a program needn't handle non-finite values.
Results may differ from the reference program's by a relative error of at most 0.025.
Values may be sent and summed in bfloat16 or wider, within the bound.
No kernel may reach another device: no remote copies, remote signals or barrier semaphores. Data moves between devices by JAX's collectives and lax.ppermute only.
A program may use at most 64 MiB of HBM per device.

```python
import math
import jax
import jax.numpy as jnp
from jax import lax

NEV = 256
LX = 32
LY = 16
SITES = 512
NS = 2048
LZ = 4
TIMES = 4
N_SPACE = 4


def with_ends(drawn, own_key, least, largest):
    place = [jax.random.randint(jax.random.fold_in(own_key, axis), (), 0, length) for axis, length in enumerate(drawn.shape)]
    longest = drawn.shape.index(max(drawn.shape))
    beside = place[:longest] + [(place[longest] + 1) % drawn.shape[longest]] + place[longest + 1:]
    return drawn.at[tuple(place)].set(least).at[tuple(beside)].set(largest)


def shard_levels(rng, extent, pieces, least, top_value):
    def one(dim, blocks):
        heights = jax.random.uniform(jax.random.fold_in(jax.random.fold_in(rng, 6), dim), (blocks,), jnp.float32, least / len(pieces), top_value / len(pieces))
        return jnp.repeat(jnp.exp(heights), extent[dim] // blocks).reshape((-1,) + (1,) * (len(extent) - dim - 1))

    loudness = one(*pieces[0])
    for cut in pieces[1:]:
        loudness = loudness * one(*cut)
    return loudness


def scatter_about(own_key, extent, spread, reach, cuts=(), held_as=jnp.bfloat16):
    level = shard_levels(own_key, extent, cuts, -0.22, 0.18) if cuts else 1.0
    array = jax.random.normal(own_key, extent, jnp.float32) * spread * level
    return jnp.minimum(jnp.maximum(array, -reach), reach).astype(held_as)


def setup_inputs(seed: int = 0, part: int = 0) -> dict:
    seeds = jax.random.split(jax.random.key(seed), 5)
    part_keys = jax.random.split(jax.random.fold_in(seeds[4], part), 5)
    eigvecs = scatter_about(part_keys[0], (TIMES, 2, 3, NS, NEV), 1.0, 6.0, ((0, 4), (3, 4)))
    links = scatter_about(part_keys[1], (TIMES, 3, 2, 3, 3, NS), 0.4, 2.5, ((0, 4), (5, 4)))
    momenta = with_ends(jax.random.randint(seeds[2], (3, 3), -2, 3), jax.random.fold_in(seeds[2], 1), -2, 2).astype(jnp.int32)
    perambulators = scatter_about(part_keys[3], (TIMES, 2, NEV, NEV), (2 * NEV) ** -0.5, 0.25, ((0, 4),))
    return {"eigvecs": eigvecs, "links": links, "momenta": momenta, "perambulators": perambulators}


def color_apply(link_pair, shifted):
    link_real = link_pair[0].astype(jnp.float32)
    link_imag = link_pair[1].astype(jnp.float32)
    moved_real = shifted[0].astype(jnp.float32)
    moved_imag = shifted[1].astype(jnp.float32)
    real_part = jnp.einsum('abs,bsm->asm', link_real, moved_real) - jnp.einsum('abs,bsm->asm', link_imag, moved_imag)
    imag_part = jnp.einsum('abs,bsm->asm', link_real, moved_imag) + jnp.einsum('abs,bsm->asm', link_imag, moved_real)
    return (real_part, imag_part)

def phase_angle(momentum, first_pos, second_pos, third_pos, depth):
    weights = momentum.astype(jnp.float32)
    return 2.0 * math.pi * (weights[0] * first_pos / LX + weights[1] * second_pos / LY + weights[2] * third_pos / depth)

def phased(real_part, imag_part, angle):
    cosine = jnp.cos(angle)[None, :, None]
    sine_value = jnp.sin(angle)[None, :, None]
    phased_real = (cosine * real_part + sine_value * imag_part).astype(jnp.bfloat16)
    phased_imag = (cosine * imag_part - sine_value * real_part).astype(jnp.bfloat16)
    upper = jnp.stack([phased_real, phased_imag], 2)
    lower = jnp.stack([phased_imag, -phased_real], 2)
    return jnp.stack([upper, lower], 0)

def section_elementals(vectors, link_set, momenta):
    lattice = vectors.reshape(2, 3, LZ, LY, LX, NEV)
    shifted = [jnp.roll(lattice, -1, 4), jnp.roll(lattice, -1, 3), jnp.roll(lattice, -1, 2)]
    site_index = jnp.arange(NS, dtype=jnp.int32)
    first_pos = (site_index % LX).astype(jnp.float32)
    second_pos = (site_index // LX % LY).astype(jnp.float32)
    third_pos = (site_index // (LX * LY)).astype(jnp.float32)
    blocks = []
    for momentum_index in range(3):
        real_part, imag_part = color_apply(link_set[momentum_index], shifted[momentum_index].reshape(2, 3, NS, NEV))
        angle = phase_angle(momenta[momentum_index], first_pos, second_pos, third_pos, LZ)
        blocks.append(phased(real_part, imag_part, angle))
    right_side = jnp.stack(blocks, 3)
    norm_factor = 1.0 / math.sqrt(6.0 * NS)

    def add_tile(running, tile_index):
        offset = tile_index * SITES
        left_block = lax.dynamic_slice_in_dim(vectors, offset, SITES, 2).reshape(6 * SITES, NEV)
        right_block = lax.dynamic_slice_in_dim(right_side, offset, SITES, 2).reshape(6 * SITES, 6 * NEV)
        partial_value = lax.dot_general(left_block, right_block, (((0,), (0,)), ((), ())), preferred_element_type=jnp.float32) * norm_factor
        rounded = lax.optimization_barrier(partial_value.astype(jnp.bfloat16))
        return (running + rounded.astype(jnp.float32), None)
    initial = jnp.zeros((NEV, 6 * NEV), jnp.float32)
    summed, _ = lax.scan(add_tile, initial, jnp.arange(N_SPACE, dtype=jnp.int32))
    return summed.astype(jnp.bfloat16).reshape(NEV, 3, 2, NEV)

def right_factor(resident):
    upper = jnp.concatenate([resident[0], resident[1]], 1)
    lower = jnp.concatenate([-resident[1], resident[0]], 1)
    return jnp.concatenate([upper, lower], 0)

def reference(eigvecs, links, momenta, perambulators):

    def one_slice(inputs_pair):
        return section_elementals(inputs_pair[0], inputs_pair[1], momenta)
    elementals = lax.map(one_slice, (eigvecs, links))

    def per_sink(resident):
        factor = right_factor(resident)

        def per_source(elemental):
            flattened = elemental.reshape(NEV * 3, 2 * NEV)
            product = jnp.dot(flattened, factor, preferred_element_type=jnp.float32)
            return product.astype(jnp.bfloat16).reshape(NEV, 3, 2, NEV)
        return lax.map(per_source, elementals)
    projected = lax.map(per_sink, perambulators)
    return (elementals, projected)
```

```python
import math

import jax
import jax.numpy as jnp
from jax import lax
from jax.sharding import PartitionSpec as P

LX = 32
LY = 16


def shifted_2(shard, axis, by):
    length = lax.axis_size(axis)
    return lax.ppermute(shard, axis, [(i, (i + by) % length) for i in range(length)])


def reduce_rows(partial, axis):
    length = lax.axis_size(axis)
    index = lax.axis_index(axis)
    rows = partial.shape[0] // length
    total = lax.dynamic_slice_in_dim(partial, index * rows, rows, 0).astype(jnp.float32)
    received = []
    for by in range(1, length):
        block = lax.dynamic_slice_in_dim(partial, (index + by) % length * rows, rows, 0)
        received.append(shifted_2(block, axis, by))
    for block in received:
        total = total + block.astype(jnp.float32)
    return total.astype(partial.dtype)


def gather_sections(shard, axis):
    length = lax.axis_size(axis)
    index = lax.axis_index(axis)
    shards = [shard] + [shifted_2(shard, axis, -by) for by in range(1, length)]
    whole = jnp.zeros((length,) + shard.shape, shard.dtype)
    for by, piece in enumerate(shards):
        whole = lax.dynamic_update_slice_in_dim(whole, piece[None], (index + by) % length, 0)
    return whole


def color_apply(link_pair, shifted):
    link_real = link_pair[0].astype(jnp.float32)
    link_imag = link_pair[1].astype(jnp.float32)
    moved_real = shifted[0]
    moved_imag = shifted[1]
    real_rows = []
    imag_rows = []
    for row_color in range(3):
        real_sum = None
        imag_sum = None
        for col_color in range(3):
            factor_real = link_real[row_color, col_color][:, None]
            factor_imag = link_imag[row_color, col_color][:, None]
            term_real = factor_real * moved_real[col_color] - factor_imag * moved_imag[col_color]
            term_imag = factor_real * moved_imag[col_color] + factor_imag * moved_real[col_color]
            real_sum = term_real if real_sum is None else real_sum + term_real
            imag_sum = term_imag if imag_sum is None else imag_sum + term_imag
        real_rows.append(real_sum)
        imag_rows.append(imag_sum)
    return (jnp.stack(real_rows, 0), jnp.stack(imag_rows, 0))


def phase_angle(momentum, first_pos, second_pos, third_pos, depth):
    weights = momentum.astype(jnp.float32)
    return (
        2.0
        * math.pi
        * (
            weights[0] * first_pos / LX
            + weights[1] * second_pos / LY
            + weights[2] * third_pos / depth
        )
    )


def phased_pair(real_part, imag_part, angle):
    cosine = jnp.cos(angle)[None, :, None]
    sine_value = jnp.sin(angle)[None, :, None]
    phased_real = (cosine * real_part + sine_value * imag_part).astype(jnp.bfloat16)
    phased_imag = (cosine * imag_part - sine_value * real_part).astype(jnp.bfloat16)
    rows = phased_real.shape[0] * phased_real.shape[1]
    width = phased_real.shape[2]
    return jnp.stack([phased_real.reshape(rows, width), phased_imag.reshape(rows, width)], 1)


def combine_parts(real_left, imag_left, right_flat):
    dims = (((0,), (0,)), ((), ()))
    from_real = lax.dot_general(real_left, right_flat, dims, preferred_element_type=jnp.float32)
    from_imag = lax.dot_general(imag_left, right_flat, dims, preferred_element_type=jnp.float32)
    return (from_real, from_imag)


def body(eigvecs, links, momenta, perambulators):
    vectors = eigvecs[0]
    link_set = links[0]
    mode_count = vectors.shape[3]
    site_count = vectors.shape[2]
    tile_count = lax.axis_size("space")
    tile_index = lax.axis_index("space")
    planes = site_count // (LX * LY)
    lattice = vectors.reshape(2, 3, planes, LY, LX, mode_count)
    forward = shifted_2(lattice[:, :, 0], "space", -1)
    site_index = jnp.arange(site_count, dtype=jnp.int32)
    first_pos = (site_index % LX).astype(jnp.float32)
    second_pos = (site_index // LX % LY).astype(jnp.float32)
    third_pos = (tile_index * planes + site_index // (LX * LY)).astype(jnp.float32)
    blocks = []
    for momentum_index in range(3):
        if momentum_index == 0:
            moved = jnp.roll(lattice, -1, 4)
        elif momentum_index == 1:
            moved = jnp.roll(lattice, -1, 3)
        else:
            moved = jnp.concatenate([lattice[:, :, 1:], forward[:, :, None]], 2)
        real_part, imag_part = color_apply(
            link_set[momentum_index], moved.reshape(2, 3, site_count, mode_count)
        )
        angle = phase_angle(
            momenta[momentum_index], first_pos, second_pos, third_pos, planes * tile_count
        )
        blocks.append(phased_pair(real_part, imag_part, angle))
    real_left = vectors[0].reshape(3 * site_count, mode_count)
    imag_left = vectors[1].reshape(3 * site_count, mode_count)
    norm_factor = 1.0 / math.sqrt(6.0 * site_count * tile_count)
    owned_rows = mode_count // tile_count
    right_flat = jnp.stack(blocks, 1).reshape(3 * site_count, 6 * mode_count)
    from_real, from_imag = combine_parts(real_left, imag_left, right_flat)
    from_real = from_real.reshape(lax.axis_size("space") * owned_rows, 3, 2, mode_count)
    from_imag = from_imag.reshape(lax.axis_size("space") * owned_rows, 3, 2, mode_count)
    real_out = from_real[:, :, 0] + from_imag[:, :, 1]
    imag_out = from_real[:, :, 1] - from_imag[:, :, 0]
    partial = (jnp.stack([real_out, imag_out], 2) * norm_factor).astype(jnp.bfloat16)
    summed = reduce_rows(partial, "space")
    resident = perambulators[0]
    factor = jnp.concatenate(
        [
            jnp.concatenate([resident[0], resident[1]], 1),
            jnp.concatenate([-resident[1], resident[0]], 1),
        ],
        0,
    )
    piece = gather_sections(summed, "tm")
    count = piece.shape[0]
    flattened = piece.reshape(count * owned_rows * 3, 2 * mode_count)
    product = jnp.dot(flattened, factor, preferred_element_type=jnp.float32)
    projected = product.astype(jnp.bfloat16).reshape(count, owned_rows, 3, 2, mode_count)
    return (summed[None], projected[None])


def solution(mesh):
    in_specs = (
        P(("ens", "tm"), None, None, "space", None),
        P(("ens", "tm"), None, None, None, None, "space"),
        P(),
        P(("ens", "tm"), None, None, None),
    )
    out_specs = (
        P(("ens", "tm"), "space", None, None, None),
        P(("ens", "tm"), None, "space", None, None, None),
    )
    return jax.shard_map(body, mesh=mesh, in_specs=in_specs, out_specs=out_specs, check_vma=False)
```

```python
import functools
import math

import jax
import jax.numpy as jnp
from jax import lax
from jax.experimental import pallas as pl
from jax.experimental.pallas import tpu as pltpu
from jax.sharding import PartitionSpec as P

LX = 32
LY = 16


def shifted_2(shard, axis, by):
    length = lax.axis_size(axis)
    return lax.ppermute(shard, axis, [(i, (i + by) % length) for i in range(length)])


def phase_angle(momentum, first_pos, second_pos, third_pos, depth):
    weights = momentum.astype(jnp.float32)
    return (
        2.0
        * math.pi
        * (
            weights[0] * first_pos / LX
            + weights[1] * second_pos / LY
            + weights[2] * third_pos / depth
        )
    )


def phased_links(links, momenta, tile_index, tile_count):
    site_count = links.shape[-1]
    planes = site_count // (LX * LY)
    site_index = jnp.arange(site_count, dtype=jnp.int32)
    first_pos = (site_index % LX).astype(jnp.float32)
    second_pos = (site_index // LX % LY).astype(jnp.float32)
    third_pos = (tile_index * planes + site_index // (LX * LY)).astype(jnp.float32)
    angle = jnp.stack(
        [phase_angle(momenta[k], first_pos, second_pos, third_pos, planes * tile_count) for k in range(3)]
    )
    cosine = jnp.cos(angle)[:, None, None]
    sine = jnp.sin(angle)[:, None, None]
    link = links.astype(jnp.float32)
    real = cosine * link[:, 0] + sine * link[:, 1]
    imag = cosine * link[:, 1] - sine * link[:, 0]
    return jnp.stack([real, imag], 3).reshape(3 * 18, site_count).T


def left_rows(vectors):
    _, colors, site_count, modes = vectors.shape
    turned = jnp.transpose(vectors, (3, 0, 1, 2)).reshape(modes, 2, colors * site_count)
    upper = turned.reshape(modes, 1, 2 * colors * site_count)
    lower = jnp.concatenate([-turned[:, 1:], turned[:, :1]], 1).reshape(upper.shape)
    return jnp.concatenate([upper, lower], 1).reshape(2 * modes, 2 * colors * site_count)


def contract_kernel(index_ref, left_ref, weights_ref, source_ref, *rest, directions, scale):
    outs, right_ref, total_ref = rest[:-2], rest[-2], rest[-1]
    sites = source_ref.shape[2]
    count = len(outs)
    rows = total_ref.shape[0] // count
    for slot, direction in enumerate(directions):

        def step(block, _):
            row = pl.multiple_of(block * LX, LX)
            if direction == 1:
                plane = block // LY * LY
                from_row = pl.multiple_of((plane + (block - plane + 1) % LY) * LX, LX)
            else:
                from_row = row
            real = [source_ref[0, b, pl.ds(from_row, LX), :].astype(jnp.float32) for b in range(3)]
            imag = [source_ref[1, b, pl.ds(from_row, LX), :].astype(jnp.float32) for b in range(3)]
            if direction == 0:
                real = [pltpu.roll(v, LX - 1, 0) for v in real]
                imag = [pltpu.roll(v, LX - 1, 0) for v in imag]
            weights = weights_ref[pl.ds(row, LX), :]
            for a in range(3):
                real_sum = None
                imag_sum = None
                for b in range(3):
                    column = ((direction * 3 + a) * 3 + b) * 2
                    w_real = weights[:, column : column + 1]
                    w_imag = weights[:, column + 1 : column + 2]
                    term_real = w_real * real[b] - w_imag * imag[b]
                    term_imag = w_real * imag[b] + w_imag * real[b]
                    real_sum = term_real if b == 0 else real_sum + term_real
                    imag_sum = term_imag if b == 0 else imag_sum + term_imag
                right_ref[pl.ds(a * sites + row, LX), :] = real_sum.astype(jnp.bfloat16)
                right_ref[pl.ds((3 + a) * sites + row, LX), :] = imag_sum.astype(jnp.bfloat16)
            return 0

        lax.fori_loop(0, sites // LX, step, 0)
        total_ref[...] = (
            jnp.dot(left_ref[...], right_ref[...], preferred_element_type=jnp.float32) * scale
        )
        for d in range(count):
            owner = (index_ref[0] + d) % count
            block = total_ref[pl.ds(pl.multiple_of(owner * rows, rows), rows), :]
            outs[d][slot] = block.astype(jnp.bfloat16)


def contract(index, left, weights, source, directions, count, scale):
    modes = source.shape[3]
    rows = 2 * modes // count
    out = jax.ShapeDtypeStruct((len(directions), rows, modes), jnp.bfloat16)
    vmem = pl.BlockSpec(memory_space=pltpu.VMEM)
    return pl.pallas_call(
        functools.partial(contract_kernel, directions=directions, scale=scale),
        out_shape=[out] * count,
        in_specs=[pl.BlockSpec(memory_space=pltpu.SMEM), vmem, vmem, vmem],
        out_specs=[vmem] * count,
        scratch_shapes=[
            pltpu.VMEM((left.shape[1], modes), jnp.bfloat16),
            pltpu.VMEM((left.shape[0], modes), jnp.float32),
        ],
        cost_estimate=pl.CostEstimate(
            flops=2 * len(directions) * left.shape[0] * left.shape[1] * modes,
            transcendentals=0,
            bytes_accessed=2 * (left.size + source.size),
        ),
        name="contract_" + "".join("xyz"[d] for d in directions),
    )(index, left, weights, source)


def owned_sum(blocks):
    total = blocks[0].astype(jnp.float32)
    for block in blocks[1:]:
        total = total + block.astype(jnp.float32)
    return total.astype(blocks[0].dtype)


def project_kernel(index_ref, factor_ref, *rest, count, groups):
    pieces, (own_ref, out_ref) = rest[:-2], rest[-2:]
    modes = factor_ref.shape[1]
    for by in range(count):
        section = (index_ref[0] + by) % count
        base = 0
        for group, size in enumerate(groups):
            piece_ref = pieces[by * len(groups) + group]
            rows = piece_ref.shape[1]
            for k in range(size):
                value = piece_ref[k]
                wide = value.astype(jnp.float32)
                even = lax.broadcasted_iota(jnp.int32, wide.shape, 0) % 2 == 0
                turned = jnp.where(even, -pltpu.roll(wide, rows - 1, 0), pltpu.roll(wide, 1, 0))
                result = jnp.dot(value, factor_ref[0], preferred_element_type=jnp.float32)
                result = result + jnp.dot(
                    turned.astype(jnp.bfloat16), factor_ref[1], preferred_element_type=jnp.float32
                )
                out_ref[section, :, base + k, :, :] = result.astype(jnp.bfloat16).reshape(
                    rows // 2, 2, modes
                )
                if by == 0:
                    own_ref[:, base + k, :, :] = value.reshape(rows // 2, 2, modes)
            base += size


def project(index, factor, pieces, count, groups):
    rows, modes = pieces[0].shape[1:]
    total = sum(groups)
    vmem = pl.BlockSpec(memory_space=pltpu.VMEM)
    return pl.pallas_call(
        functools.partial(project_kernel, count=count, groups=groups),
        out_shape=[
            jax.ShapeDtypeStruct((rows // 2, total, 2, modes), jnp.bfloat16),
            jax.ShapeDtypeStruct((count, rows // 2, total, 2, modes), jnp.bfloat16),
        ],
        in_specs=[pl.BlockSpec(memory_space=pltpu.SMEM)] + [vmem] * (1 + len(pieces)),
        out_specs=[vmem, vmem],
        name="project",
    )(index, factor, *pieces)


def exchange(blocks, axis):
    received = [shifted_2(blocks[by], axis, by) for by in range(1, len(blocks))]
    return owned_sum([blocks[0]] + received)


def gather(shard, axis):
    return [shard] + [shifted_2(shard, axis, -by) for by in range(1, lax.axis_size(axis))]


def body(eigvecs, links, momenta, perambulators):
    vectors = eigvecs[0]
    _, colors, site_count, mode_count = vectors.shape
    tile_count = lax.axis_size("space")
    tile_index = lax.axis_index("space")
    section_count = lax.axis_size("tm")
    plane = LX * LY
    forward = shifted_2(vectors[:, :, :plane], "space", -1)
    scale = 1.0 / math.sqrt(6.0 * site_count * tile_count)
    weights = phased_links(links[0], momenta, tile_index, tile_count)
    left = left_rows(vectors)
    tile = tile_index.astype(jnp.int32).reshape(1)
    flat = contract(tile, left, weights, vectors, (0, 1), tile_count, scale)
    raised = jnp.concatenate([vectors[:, :, plane:], forward], 2)
    deep = contract(tile, left, weights, raised, (2,), tile_count, scale)
    flat_sum = exchange(flat, "space")
    deep_sum = exchange(deep, "space")
    pieces = []
    for pair in zip(gather(flat_sum, "tm"), gather(deep_sum, "tm")):
        pieces += list(pair)
    section = lax.axis_index("tm").astype(jnp.int32).reshape(1)
    own, projected = project(section, perambulators[0], pieces, section_count, (2, 1))
    return (own[None], projected[None])


def solution(mesh):
    in_specs = (
        P(("ens", "tm"), None, None, "space", None),
        P(("ens", "tm"), None, None, None, None, "space"),
        P(),
        P(("ens", "tm"), None, None, None),
    )
    out_specs = (
        P(("ens", "tm"), "space", None, None, None),
        P(("ens", "tm"), None, "space", None, None, None),
    )
    return jax.shard_map(body, mesh=mesh, in_specs=in_specs, out_specs=out_specs, check_vma=False)
```

```python
import functools
import math

import jax
import jax.numpy as jnp
from jax import lax
from jax.experimental import pallas as pl
from jax.experimental.pallas import tpu as pltpu
from jax.sharding import PartitionSpec as P

LX = 32
LY = 16
PARTS = 4


def shifted_2(shard, axis, by):
    length = lax.axis_size(axis)
    return lax.ppermute(shard, axis, [(i, (i + by) % length) for i in range(length)])


def phase_angle(momentum, first_pos, second_pos, third_pos, depth):
    weights = momentum.astype(jnp.float32)
    return (
        2.0
        * math.pi
        * (
            weights[0] * first_pos / LX
            + weights[1] * second_pos / LY
            + weights[2] * third_pos / depth
        )
    )


def phased_links(links, momenta, tile_index, tile_count):
    site_count = links.shape[-1]
    planes = site_count // (LX * LY)
    site_index = jnp.arange(site_count, dtype=jnp.int32)
    first_pos = (site_index % LX).astype(jnp.float32)
    second_pos = (site_index // LX % LY).astype(jnp.float32)
    third_pos = (tile_index * planes + site_index // (LX * LY)).astype(jnp.float32)
    angle = jnp.stack(
        [phase_angle(momenta[k], first_pos, second_pos, third_pos, planes * tile_count) for k in range(3)]
    )
    cosine = jnp.cos(angle)[:, None, None]
    sine = jnp.sin(angle)[:, None, None]
    link = links.astype(jnp.float32)
    real = cosine * link[:, 0] + sine * link[:, 1]
    imag = cosine * link[:, 1] - sine * link[:, 0]
    return jnp.stack([real, imag], 3).reshape(3 * 18, site_count).T


def left_rows(source_ref, left_ref):
    _, colors, sites, modes = source_ref.shape
    share = sites // PARTS
    shape = (2 * modes, 2 * modes)
    row = lax.broadcasted_iota(jnp.int32, shape, 0)
    column = lax.broadcasted_iota(jnp.int32, shape, 1)
    one = jnp.ones(shape, jnp.float32)
    zero = jnp.zeros(shape, jnp.float32)
    first = jnp.where(row == 2 * column, one, zero)
    first = first - jnp.where(row == 2 * (column - modes) + 1, one, zero)
    second = jnp.where(row == 2 * column + 1, one, zero)
    second = second + jnp.where(row == 2 * (column - modes), one, zero)
    picks = (first.astype(jnp.bfloat16), second.astype(jnp.bfloat16))
    width = colors * share
    for part in range(PARTS):
        pair = jnp.concatenate(
            [
                source_ref[r, :, part * share : (part + 1) * share, :].reshape(width, modes)
                for r in range(2)
            ],
            1,
        )
        for r in range(2):
            turned = lax.dot_general(
                picks[r], pair, (((1,), (1,)), ((), ())), preferred_element_type=jnp.float32
            )
            start = (part * 2 + r) * width
            left_ref[:, start : start + width] = turned.astype(jnp.bfloat16)


def right_row(block, r, a, share):
    part = block // (share // LX)
    return ((part * 2 + r) * 3 + a - part) * share + block * LX


def color_sum(weight, real, imag, a):
    real_sum = None
    imag_sum = None
    for b in range(3):
        w_real, w_imag = weight(a, b, 0), weight(a, b, 1)
        term_real = w_real * real[b] - w_imag * imag[b]
        term_imag = w_real * imag[b] + w_imag * real[b]
        real_sum = term_real if b == 0 else real_sum + term_real
        imag_sum = term_imag if b == 0 else imag_sum + term_imag
    return real_sum, imag_sum


def store_owned(index_ref, total_ref, outs, slot):
    count = len(outs)
    rows = total_ref.shape[0] // count
    for d in range(count):
        owner = (index_ref[0] + d) % count
        block = total_ref[pl.ds(pl.multiple_of(owner * rows, rows), rows), :]
        outs[d][slot] = block.astype(jnp.bfloat16)


def flat_kernel(index_ref, weights_ref, source_ref, *rest, scale):
    outs, left_ref, wide_ref, right_ref, total_ref = rest[:-4], *rest[-4:]
    sites = source_ref.shape[2]
    share = sites // PARTS
    left_rows(source_ref, left_ref)
    for direction in range(2):

        def step(block, _):
            row = pl.multiple_of(block * LX, LX)
            from_row = row
            if direction == 1:
                plane = block // LY * LY
                from_row = pl.multiple_of((plane + (block - plane + 1) % LY) * LX, LX)
            parts = [
                [source_ref[r, b, pl.ds(from_row, LX), :].astype(jnp.float32) for b in range(3)]
                for r in range(2)
            ]
            if direction == 0:
                parts = [[pltpu.roll(v, LX - 1, 0) for v in part] for part in parts]
            weights = weights_ref[pl.ds(row, LX), :]

            def weight(a, b, r, k=direction):
                column = ((k * 3 + a) * 3 + b) * 2 + r
                return weights[:, column : column + 1]

            for a in range(3):
                for r, value in enumerate(color_sum(weight, *parts, a)):
                    start = pl.multiple_of(right_row(block, r, a, share), LX)
                    right_ref[pl.ds(start, LX), :] = value.astype(jnp.bfloat16)
            if direction == 0:
                for column in range(18):
                    value = weight(0, 0, column, 2).astype(jnp.bfloat16)
                    wide_ref[column, pl.ds(row, LX), :] = jnp.broadcast_to(value, (LX, 128))
            return 0

        lax.fori_loop(0, sites // LX, step, 0)
        total_ref[...] = (
            jnp.dot(left_ref[...], right_ref[...], preferred_element_type=jnp.float32) * scale
        )
        store_owned(index_ref, total_ref, outs, direction)


def deep_kernel(index_ref, left_ref, wide_ref, source_ref, *rest, scale):
    outs, buffer_ref, right_ref, total_ref, sems = rest[:-4], *rest[-4:]
    sites = source_ref.shape[2]
    share = sites // PARTS
    width = left_ref.shape[1] // PARTS
    modes = source_ref.shape[3]
    copies = []
    for part in range(PARTS):
        rows = pl.ds(part * share, share)
        copies.append(
            pltpu.make_async_copy(
                source_ref.at[:, :, rows, :], buffer_ref.at[:, :, rows, :], sems.at[part]
            )
        )
        copies[-1].start()
    for part in range(PARTS):
        copies[part].wait()
        for block in range(part * share // LX, (part + 1) * share // LX):
            row = block * LX
            for lane in range(0, modes, 128):
                real, imag = [
                    [buffer_ref[r, b, row : row + LX, lane : lane + 128] for b in range(3)]
                    for r in range(2)
                ]

                def weight(a, b, r):
                    return wide_ref[(a * 3 + b) * 2 + r, row : row + LX, :]

                for a in range(3):
                    for r, value in enumerate(color_sum(weight, real, imag, a)):
                        start = right_row(block, r, a, share)
                        right_ref[start : start + LX, lane : lane + 128] = value
        value = jnp.dot(
            left_ref[:, part * width : (part + 1) * width],
            right_ref[part * width : (part + 1) * width, :],
            preferred_element_type=jnp.float32,
        )
        if part:
            value = total_ref[...] + value
        if part == PARTS - 1:
            value = value * scale
        total_ref[...] = value
    store_owned(index_ref, total_ref, outs, 0)


def contract_flat(index, weights, vectors, count, scale):
    _, colors, sites, modes = vectors.shape
    depth = 2 * colors * sites
    out = jax.ShapeDtypeStruct((2, 2 * modes // count, modes), jnp.bfloat16)
    vmem = pl.BlockSpec(memory_space=pltpu.VMEM)
    return pl.pallas_call(
        functools.partial(flat_kernel, scale=scale),
        out_shape=[out] * count
        + [
            pltpu.VMEM((2 * modes, depth), jnp.bfloat16),
            pltpu.VMEM((18, sites, 128), jnp.bfloat16),
        ],
        in_specs=[pl.BlockSpec(memory_space=pltpu.SMEM), vmem, vmem],
        out_specs=[vmem] * (count + 2),
        scratch_shapes=[
            pltpu.VMEM((depth, modes), jnp.bfloat16),
            pltpu.VMEM((2 * modes, modes), jnp.float32),
        ],
        cost_estimate=pl.CostEstimate(
            flops=12 * modes * depth * modes, transcendentals=0, bytes_accessed=4 * depth * modes
        ),
        compiler_params=pltpu.CompilerParams(vmem_limit_bytes=24 << 20),
        name="contract_xy",
    )(index, weights, vectors)


def contract_deep(index, left, wide, source, count, scale):
    _, colors, sites, modes = source.shape
    depth = 2 * colors * sites
    out = jax.ShapeDtypeStruct((1, 2 * modes // count, modes), jnp.bfloat16)
    vmem = pl.BlockSpec(memory_space=pltpu.VMEM)
    return pl.pallas_call(
        functools.partial(deep_kernel, scale=scale),
        out_shape=[out] * count,
        in_specs=[
            pl.BlockSpec(memory_space=pltpu.SMEM),
            vmem,
            vmem,
            pl.BlockSpec(memory_space=pl.ANY),
        ],
        out_specs=[vmem] * count,
        scratch_shapes=[
            pltpu.VMEM(source.shape, jnp.bfloat16),
            pltpu.VMEM((depth, modes), jnp.bfloat16),
            pltpu.VMEM((2 * modes, modes), jnp.float32),
            pltpu.SemaphoreType.DMA((PARTS,)),
        ],
        cost_estimate=pl.CostEstimate(
            flops=4 * modes * depth * modes, transcendentals=0, bytes_accessed=2 * depth * modes
        ),
        compiler_params=pltpu.CompilerParams(vmem_limit_bytes=24 << 20),
        name="contract_z",
    )(
        index,
        pltpu.with_memory_space_constraint(left, pltpu.VMEM),
        pltpu.with_memory_space_constraint(wide, pltpu.VMEM),
        source,
    )


def owned_sum(blocks):
    total = blocks[0].astype(jnp.float32)
    for block in blocks[1:]:
        total = total + block.astype(jnp.float32)
    return total.astype(blocks[0].dtype)


def project_kernel(index_ref, factor_ref, *rest, count):
    pieces, (own_ref, out_ref) = rest[:count], rest[-2:]
    size, rows, modes = pieces[0].shape
    even = lax.broadcasted_iota(jnp.int32, (rows, modes), 0) % 2 == 0
    for by in range(count):
        section = (index_ref[0] + by) % count
        for k in range(size):
            value = pieces[by][k]
            wide = value.astype(jnp.float32)
            turned = jnp.where(even, -pltpu.roll(wide, rows - 1, 0), pltpu.roll(wide, 1, 0))
            result = jnp.dot(value, factor_ref[0], preferred_element_type=jnp.float32)
            result = result + jnp.dot(
                turned.astype(jnp.bfloat16), factor_ref[1], preferred_element_type=jnp.float32
            )
            out_ref[section, :, k, :, :] = result.astype(jnp.bfloat16).reshape(rows // 2, 2, modes)
            if by == 0:
                own_ref[:, k, :, :] = value.reshape(rows // 2, 2, modes)


def project(index, factor, pieces, total, first, earlier):
    count = len(pieces)
    size, rows, modes = pieces[0].shape
    vmem = pl.BlockSpec(memory_space=pltpu.VMEM)
    kept = pl.BlockSpec(memory_space=pl.ANY)
    step = first // size
    return pl.pallas_call(
        functools.partial(project_kernel, count=count),
        grid=(1,),
        out_shape=[
            jax.ShapeDtypeStruct((rows // 2, total, 2, modes), jnp.bfloat16),
            jax.ShapeDtypeStruct((count, rows // 2, total, 2, modes), jnp.bfloat16),
        ],
        in_specs=[pl.BlockSpec(memory_space=pltpu.SMEM)]
        + [vmem] * (1 + count)
        + [kept] * len(earlier),
        out_specs=[
            pl.BlockSpec((rows // 2, size, 2, modes), lambda i: (0, step, 0, 0)),
            pl.BlockSpec((count, rows // 2, size, 2, modes), lambda i: (0, 0, step, 0, 0)),
        ],
        input_output_aliases={2 + count + i: i for i in range(len(earlier))},
        name="project_%d" % first,
    )(index, factor, *pieces, *earlier)


def exchange(blocks, axis):
    return [blocks[0]] + [shifted_2(blocks[by], axis, by) for by in range(1, len(blocks))]


def gather(shard, axis):
    return [shard] + [shifted_2(shard, axis, -by) for by in range(1, lax.axis_size(axis))]


def body(eigvecs, links, momenta, perambulators):
    vectors = eigvecs[0]
    _, colors, site_count, mode_count = vectors.shape
    tile_count = lax.axis_size("space")
    tile_index = lax.axis_index("space")
    plane = LX * LY
    forward = shifted_2(vectors[:, :, :plane], "space", -1)
    scale = 1.0 / math.sqrt(6.0 * site_count * tile_count)
    weights = phased_links(links[0], momenta, tile_index, tile_count)
    tile = tile_index.astype(jnp.int32).reshape(1)
    section = lax.axis_index("tm").astype(jnp.int32).reshape(1)
    *flat, left, wide = contract_flat(tile, weights, vectors, tile_count, scale)
    raised = jnp.concatenate([vectors[:, :, plane:], forward], 2)
    flat_parts = exchange(flat, "space")
    deep = contract_deep(tile, left, wide, raised, tile_count, scale)
    flat_parts, _ = lax.optimization_barrier((flat_parts, deep))
    deep_parts = exchange(deep, "space")
    factor = perambulators[0]
    flat_pieces = gather(owned_sum(flat_parts), "tm")
    earlier = project(section, factor, flat_pieces, 3, 0, ())
    deep_pieces = gather(owned_sum(deep_parts), "tm")
    own, projected = project(section, factor, deep_pieces, 3, 2, earlier)
    return (own[None], projected[None])


def solution(mesh):
    in_specs = (
        P(("ens", "tm"), None, None, "space", None),
        P(("ens", "tm"), None, None, None, None, "space"),
        P(),
        P(("ens", "tm"), None, None, None),
    )
    out_specs = (
        P(("ens", "tm"), "space", None, None, None),
        P(("ens", "tm"), None, "space", None, None, None),
    )
    return jax.shard_map(body, mesh=mesh, in_specs=in_specs, out_specs=out_specs, check_vma=False)
```

```python
import functools
import math

import jax
import jax.numpy as jnp
from jax import lax
from jax.experimental import pallas as pl
from jax.experimental.pallas import tpu as pltpu
from jax.sharding import PartitionSpec as P

LX = 32
LY = 16
PARTS = 4


def shifted_2(shard, axis, by):
    length = lax.axis_size(axis)
    return lax.ppermute(shard, axis, [(i, (i + by) % length) for i in range(length)])


def phase_angle(momentum, first_pos, second_pos, third_pos, depth):
    weights = momentum.astype(jnp.float32)
    return (
        2.0
        * math.pi
        * (
            weights[0] * first_pos / LX
            + weights[1] * second_pos / LY
            + weights[2] * third_pos / depth
        )
    )


def phased_links(links, momenta, tile_index, tile_count):
    site_count = links.shape[-1]
    planes = site_count // (LX * LY)
    site_index = jnp.arange(site_count, dtype=jnp.int32)
    first_pos = (site_index % LX).astype(jnp.float32)
    second_pos = (site_index // LX % LY).astype(jnp.float32)
    third_pos = (tile_index * planes + site_index // (LX * LY)).astype(jnp.float32)
    angle = jnp.stack(
        [phase_angle(momenta[k], first_pos, second_pos, third_pos, planes * tile_count) for k in range(3)]
    )
    cosine = jnp.cos(angle)[:, None, None]
    sine = jnp.sin(angle)[:, None, None]
    link = links.astype(jnp.float32)
    real = cosine * link[:, 0] + sine * link[:, 1]
    imag = cosine * link[:, 1] - sine * link[:, 0]
    return jnp.stack([real, imag], 3).reshape(3 * 18, site_count).T


def left_rows(source_ref, left_ref):
    _, colors, sites, modes = source_ref.shape
    share = sites // PARTS
    shape = (2 * modes, 2 * modes)
    row = lax.broadcasted_iota(jnp.int32, shape, 0)
    column = lax.broadcasted_iota(jnp.int32, shape, 1)
    one = jnp.ones(shape, jnp.float32)
    zero = jnp.zeros(shape, jnp.float32)
    first = jnp.where(row == 2 * column, one, zero)
    first = first - jnp.where(row == 2 * (column - modes) + 1, one, zero)
    second = jnp.where(row == 2 * column + 1, one, zero)
    second = second + jnp.where(row == 2 * (column - modes), one, zero)
    picks = (first.astype(jnp.bfloat16), second.astype(jnp.bfloat16))
    width = colors * share
    for part in range(PARTS):
        pair = jnp.concatenate(
            [
                source_ref[r, :, part * share : (part + 1) * share, :].reshape(width, modes)
                for r in range(2)
            ],
            1,
        )
        for r in range(2):
            turned = lax.dot_general(
                picks[r], pair, (((1,), (1,)), ((), ())), preferred_element_type=jnp.float32
            )
            start = (part * 2 + r) * width
            left_ref[:, start : start + width] = turned.astype(jnp.bfloat16)


def right_row(block, r, a, share):
    part = block // (share // LX)
    return ((part * 2 + r) * 3 + a - part) * share + block * LX


def color_sum(weight, real, imag, a):
    real_sum = None
    imag_sum = None
    for b in range(3):
        w_real, w_imag = weight(a, b, 0), weight(a, b, 1)
        term_real = w_real * real[b] - w_imag * imag[b]
        term_imag = w_real * imag[b] + w_imag * real[b]
        real_sum = term_real if b == 0 else real_sum + term_real
        imag_sum = term_imag if b == 0 else imag_sum + term_imag
    return real_sum, imag_sum


def store_owned(index_ref, total_ref, outs, slot):
    count = len(outs)
    rows = total_ref.shape[0] // count
    for d in range(count):
        owner = (index_ref[0] + d) % count
        block = total_ref[pl.ds(pl.multiple_of(owner * rows, rows), rows), :]
        outs[d][slot] = block.astype(jnp.bfloat16)


def flat_kernel(index_ref, weights_ref, source_ref, *rest, scale):
    outs, left_ref, wide_ref, right_ref, total_ref = rest[:-4], *rest[-4:]
    sites = source_ref.shape[2]
    share = sites // PARTS
    left_rows(source_ref, left_ref)
    for direction in range(2):

        def step(block, _):
            row = pl.multiple_of(block * LX, LX)
            from_row = row
            if direction == 1:
                plane = block // LY * LY
                from_row = pl.multiple_of((plane + (block - plane + 1) % LY) * LX, LX)
            parts = [
                [source_ref[r, b, pl.ds(from_row, LX), :].astype(jnp.float32) for b in range(3)]
                for r in range(2)
            ]
            if direction == 0:
                parts = [[pltpu.roll(v, LX - 1, 0) for v in part] for part in parts]
            weights = weights_ref[pl.ds(row, LX), :]

            def weight(a, b, r, k=direction):
                column = ((k * 3 + a) * 3 + b) * 2 + r
                return weights[:, column : column + 1]

            for a in range(3):
                for r, value in enumerate(color_sum(weight, *parts, a)):
                    start = pl.multiple_of(right_row(block, r, a, share), LX)
                    right_ref[pl.ds(start, LX), :] = value.astype(jnp.bfloat16)
            if direction == 0:
                for column in range(18):
                    value = weight(0, 0, column, 2).astype(jnp.bfloat16)
                    wide_ref[column, pl.ds(row, LX), :] = jnp.broadcast_to(value, (LX, 128))
            return 0

        lax.fori_loop(0, sites // LX, step, 0)
        total_ref[...] = (
            jnp.dot(left_ref[...], right_ref[...], preferred_element_type=jnp.float32) * scale
        )
        store_owned(index_ref, total_ref, outs, direction)


def deep_kernel(index_ref, left_ref, wide_ref, source_ref, *rest, scale):
    outs, buffer_ref, right_ref, total_ref, sems = rest[:-4], *rest[-4:]
    sites = source_ref.shape[2]
    share = sites // PARTS
    width = left_ref.shape[1] // PARTS
    modes = source_ref.shape[3]
    copies = []
    for part in range(PARTS):
        rows = pl.ds(part * share, share)
        copies.append(
            pltpu.make_async_copy(
                source_ref.at[:, :, rows, :], buffer_ref.at[:, :, rows, :], sems.at[part]
            )
        )
        copies[-1].start()
    for part in range(PARTS):
        copies[part].wait()
        for block in range(part * share // LX, (part + 1) * share // LX):
            row = block * LX
            for lane in range(0, modes, 128):
                real, imag = [
                    [buffer_ref[r, b, row : row + LX, lane : lane + 128] for b in range(3)]
                    for r in range(2)
                ]

                def weight(a, b, r):
                    return wide_ref[(a * 3 + b) * 2 + r, row : row + LX, :]

                for a in range(3):
                    for r, value in enumerate(color_sum(weight, real, imag, a)):
                        start = right_row(block, r, a, share)
                        right_ref[start : start + LX, lane : lane + 128] = value
        value = jnp.dot(
            left_ref[:, part * width : (part + 1) * width],
            right_ref[part * width : (part + 1) * width, :],
            preferred_element_type=jnp.float32,
        )
        if part:
            value = total_ref[...] + value
        if part == PARTS - 1:
            value = value * scale
        total_ref[...] = value
    store_owned(index_ref, total_ref, outs, 0)


def contract_flat(index, weights, vectors, count, scale):
    _, colors, sites, modes = vectors.shape
    depth = 2 * colors * sites
    out = jax.ShapeDtypeStruct((2, 2 * modes // count, modes), jnp.bfloat16)
    vmem = pl.BlockSpec(memory_space=pltpu.VMEM)
    return pl.pallas_call(
        functools.partial(flat_kernel, scale=scale),
        out_shape=[out] * count
        + [
            pltpu.VMEM((2 * modes, depth), jnp.bfloat16),
            pltpu.VMEM((18, sites, 128), jnp.bfloat16),
        ],
        in_specs=[pl.BlockSpec(memory_space=pltpu.SMEM), vmem, vmem],
        out_specs=[vmem] * (count + 2),
        scratch_shapes=[
            pltpu.VMEM((depth, modes), jnp.bfloat16),
            pltpu.VMEM((2 * modes, modes), jnp.float32),
        ],
        cost_estimate=pl.CostEstimate(
            flops=12 * modes * depth * modes, transcendentals=0, bytes_accessed=4 * depth * modes
        ),
        compiler_params=pltpu.CompilerParams(vmem_limit_bytes=24 << 20),
        name="contract_xy",
    )(index, weights, vectors)


def contract_deep(index, left, wide, source, count, scale):
    _, colors, sites, modes = source.shape
    depth = 2 * colors * sites
    out = jax.ShapeDtypeStruct((1, 2 * modes // count, modes), jnp.bfloat16)
    vmem = pl.BlockSpec(memory_space=pltpu.VMEM)
    return pl.pallas_call(
        functools.partial(deep_kernel, scale=scale),
        out_shape=[out] * count,
        in_specs=[
            pl.BlockSpec(memory_space=pltpu.SMEM),
            vmem,
            vmem,
            pl.BlockSpec(memory_space=pl.ANY),
        ],
        out_specs=[vmem] * count,
        scratch_shapes=[
            pltpu.VMEM(source.shape, jnp.bfloat16),
            pltpu.VMEM((depth, modes), jnp.bfloat16),
            pltpu.VMEM((2 * modes, modes), jnp.float32),
            pltpu.SemaphoreType.DMA((PARTS,)),
        ],
        cost_estimate=pl.CostEstimate(
            flops=4 * modes * depth * modes, transcendentals=0, bytes_accessed=2 * depth * modes
        ),
        compiler_params=pltpu.CompilerParams(vmem_limit_bytes=24 << 20),
        name="contract_z",
    )(
        index,
        in_vmem(left),
        in_vmem(wide),
        source,
    )


def owned_sum(blocks):
    total = blocks[0].astype(jnp.float32)
    for block in blocks[1:]:
        total = total + block.astype(jnp.float32)
    return total.astype(blocks[0].dtype)


def project_kernel(index_ref, factor_ref, *rest, count):
    pieces, (own_ref, out_ref) = rest[:count], rest[-2:]
    size, rows, modes = pieces[0].shape
    even = lax.broadcasted_iota(jnp.int32, (rows, modes), 0) % 2 == 0
    for by in range(count):
        section = (index_ref[0] + by) % count
        for k in range(size):
            value = pieces[by][k]
            wide = value.astype(jnp.float32)
            turned = jnp.where(even, -pltpu.roll(wide, rows - 1, 0), pltpu.roll(wide, 1, 0))
            result = jnp.dot(value, factor_ref[0], preferred_element_type=jnp.float32)
            result = result + jnp.dot(
                turned.astype(jnp.bfloat16), factor_ref[1], preferred_element_type=jnp.float32
            )
            out_ref[section, :, k, :, :] = result.astype(jnp.bfloat16).reshape(rows // 2, 2, modes)
            if by == 0:
                own_ref[:, k, :, :] = value.reshape(rows // 2, 2, modes)


def in_vmem(value):
    return pltpu.with_memory_space_constraint(value, pltpu.VMEM)


def project(index, factor, pieces, total, first, earlier):
    count = len(pieces)
    size, rows, modes = pieces[0].shape
    vmem = pl.BlockSpec(memory_space=pltpu.VMEM)
    kept = pl.BlockSpec(memory_space=pl.ANY)
    step = first // size
    return pl.pallas_call(
        functools.partial(project_kernel, count=count),
        grid=(1,),
        out_shape=[
            jax.ShapeDtypeStruct((rows // 2, total, 2, modes), jnp.bfloat16),
            jax.ShapeDtypeStruct((count, rows // 2, total, 2, modes), jnp.bfloat16),
        ],
        in_specs=[pl.BlockSpec(memory_space=pltpu.SMEM)]
        + [vmem] * (1 + count)
        + [kept] * len(earlier),
        out_specs=[
            pl.BlockSpec((rows // 2, size, 2, modes), lambda i: (0, step, 0, 0)),
            pl.BlockSpec((count, rows // 2, size, 2, modes), lambda i: (0, 0, step, 0, 0)),
        ],
        input_output_aliases={2 + count + i: i for i in range(len(earlier))},
    )(index, *[in_vmem(v) for v in (factor, *pieces)], *earlier)


def exchange(blocks, axis):
    return [blocks[0]] + [shifted_2(blocks[by], axis, by) for by in range(1, len(blocks))]


def gather(shard, axis):
    return [shard] + [shifted_2(shard, axis, -by) for by in range(1, lax.axis_size(axis))]


def body(eigvecs, links, momenta, perambulators):
    vectors = eigvecs[0]
    _, _, site_count, _ = vectors.shape
    tile_count = lax.axis_size("space")
    tile_index = lax.axis_index("space")
    plane = LX * LY
    forward = shifted_2(vectors[:, :, :plane], "space", -1)
    scale = 1.0 / math.sqrt(6.0 * site_count * tile_count)
    weights = phased_links(links[0], momenta, tile_index, tile_count)
    tile = tile_index.astype(jnp.int32).reshape(1)
    section = lax.axis_index("tm").astype(jnp.int32).reshape(1)
    *flat, left, wide = contract_flat(tile, weights, vectors, tile_count, scale)
    raised = jnp.concatenate([vectors[:, :, plane:], forward], 2)
    flat_parts = exchange(flat, "space")
    deep = contract_deep(tile, left, wide, raised, tile_count, scale)
    flat_parts, _ = lax.optimization_barrier((flat_parts, deep))
    deep_parts = exchange(deep, "space")
    factor = perambulators[0]
    flat_pieces = gather(owned_sum(flat_parts), "tm")
    earlier = project(section, factor, flat_pieces, 3, 0, ())
    deep_sum = owned_sum(deep_parts)
    deep_pieces = gather(deep_sum, "tm")
    own, projected = project(section, factor, deep_pieces, 3, 2, earlier)
    return (own[None], projected[None])


def solution(mesh):
    in_specs = (
        P(("ens", "tm"), None, None, "space", None),
        P(("ens", "tm"), None, None, None, None, "space"),
        P(),
        P(("ens", "tm"), None, None, None),
    )
    out_specs = (
        P(("ens", "tm"), "space", None, None, None),
        P(("ens", "tm"), None, "space", None, None, None),
    )
    return jax.shard_map(body, mesh=mesh, in_specs=in_specs, out_specs=out_specs, check_vma=False)
```

```python
import functools
import math

import jax
import jax.numpy as jnp
from jax import lax
from jax.experimental import pallas as pl
from jax.experimental.pallas import tpu as pltpu
from jax.sharding import PartitionSpec as P

LX = 32
LY = 16
PARTS = 4


def shifted_2(shard, axis, by):
    length = lax.axis_size(axis)
    return lax.ppermute(shard, axis, [(i, (i + by) % length) for i in range(length)])


def phase_angle(momentum, first_pos, second_pos, third_pos, depth):
    weights = momentum.astype(jnp.float32)
    return (
        2.0
        * math.pi
        * (
            weights[0] * first_pos / LX
            + weights[1] * second_pos / LY
            + weights[2] * third_pos / depth
        )
    )


def phased_links(links, momenta, tile_index, tile_count):
    site_count = links.shape[-1]
    planes = site_count // (LX * LY)
    site_index = jnp.arange(site_count, dtype=jnp.int32)
    first_pos = (site_index % LX).astype(jnp.float32)
    second_pos = (site_index // LX % LY).astype(jnp.float32)
    third_pos = (tile_index * planes + site_index // (LX * LY)).astype(jnp.float32)
    angle = jnp.stack(
        [phase_angle(momenta[k], first_pos, second_pos, third_pos, planes * tile_count) for k in range(3)]
    )
    cosine = jnp.cos(angle)[:, None, None]
    sine = jnp.sin(angle)[:, None, None]
    link = links.astype(jnp.float32)
    real = cosine * link[:, 0] + sine * link[:, 1]
    imag = cosine * link[:, 1] - sine * link[:, 0]
    return jnp.stack([real, imag], 3).reshape(3 * 18, site_count).T


def left_rows(source_ref, left_ref):
    _, colors, sites, modes = source_ref.shape
    share = sites // PARTS
    shape = (2 * modes, 2 * modes)
    row = lax.broadcasted_iota(jnp.int32, shape, 0)
    column = lax.broadcasted_iota(jnp.int32, shape, 1)
    one = jnp.ones(shape, jnp.float32)
    zero = jnp.zeros(shape, jnp.float32)
    first = jnp.where(row == 2 * column, one, zero)
    first = first - jnp.where(row == 2 * (column - modes) + 1, one, zero)
    second = jnp.where(row == 2 * column + 1, one, zero)
    second = second + jnp.where(row == 2 * (column - modes), one, zero)
    picks = (first.astype(jnp.bfloat16), second.astype(jnp.bfloat16))
    width = colors * share
    for part in range(PARTS):
        pair = jnp.concatenate(
            [
                source_ref[r, :, part * share : (part + 1) * share, :].reshape(width, modes)
                for r in range(2)
            ],
            1,
        )
        for r in range(2):
            turned = lax.dot_general(
                picks[r], pair, (((1,), (1,)), ((), ())), preferred_element_type=jnp.float32
            )
            start = (part * 2 + r) * width
            left_ref[:, start : start + width] = turned.astype(jnp.bfloat16)


def right_row(block, r, a, share):
    part = block // (share // LX)
    return ((part * 2 + r) * 3 + a - part) * share + block * LX


def color_sum(weight, real, imag, a):
    real_sum = None
    imag_sum = None
    for b in range(3):
        w_real, w_imag = weight(a, b, 0), weight(a, b, 1)
        term_real = w_real * real[b] - w_imag * imag[b]
        term_imag = w_real * imag[b] + w_imag * real[b]
        real_sum = term_real if b == 0 else real_sum + term_real
        imag_sum = term_imag if b == 0 else imag_sum + term_imag
    return real_sum, imag_sum


def store_owned(index_ref, total_ref, outs, slot):
    count = len(outs)
    rows = total_ref.shape[0] // count
    for d in range(count):
        owner = (index_ref[0] + d) % count
        block = total_ref[pl.ds(pl.multiple_of(owner * rows, rows), rows), :]
        outs[d][slot] = block.astype(jnp.bfloat16)


def flat_kernel(index_ref, weights_ref, source_ref, *rest, scale):
    outs, left_ref, wide_ref, right_ref, total_ref = rest[:-4], *rest[-4:]
    sites = source_ref.shape[2]
    share = sites // PARTS
    left_rows(source_ref, left_ref)
    for direction in range(2):

        def step(block, _):
            row = pl.multiple_of(block * LX, LX)
            from_row = row
            if direction == 1:
                plane = block // LY * LY
                from_row = pl.multiple_of((plane + (block - plane + 1) % LY) * LX, LX)
            parts = [
                [source_ref[r, b, pl.ds(from_row, LX), :].astype(jnp.float32) for b in range(3)]
                for r in range(2)
            ]
            if direction == 0:
                parts = [[pltpu.roll(v, LX - 1, 0) for v in part] for part in parts]
            weights = weights_ref[pl.ds(row, LX), :]

            def weight(a, b, r, k=direction):
                column = ((k * 3 + a) * 3 + b) * 2 + r
                return weights[:, column : column + 1]

            for a in range(3):
                for r, value in enumerate(color_sum(weight, *parts, a)):
                    start = pl.multiple_of(right_row(block, r, a, share), LX)
                    right_ref[pl.ds(start, LX), :] = value.astype(jnp.bfloat16)
            if direction == 0:
                for column in range(18):
                    value = weight(0, 0, column, 2).astype(jnp.bfloat16)
                    wide_ref[column, pl.ds(row, LX), :] = jnp.broadcast_to(value, (LX, 128))
            return 0

        lax.fori_loop(0, sites // LX, step, 0)
        total_ref[...] = (
            jnp.dot(left_ref[...], right_ref[...], preferred_element_type=jnp.float32) * scale
        )
        store_owned(index_ref, total_ref, outs, direction)


def deep_kernel(index_ref, left_ref, wide_ref, source_ref, *rest, scale):
    outs, buffer_ref, right_ref, total_ref, sems = rest[:-4], *rest[-4:]
    sites = source_ref.shape[2]
    share = sites // PARTS
    width = left_ref.shape[1] // PARTS
    modes = source_ref.shape[3]
    copies = []
    for part in range(PARTS):
        rows = pl.ds(part * share, share)
        copies.append(
            pltpu.make_async_copy(
                source_ref.at[:, :, rows, :], buffer_ref.at[:, :, rows, :], sems.at[part]
            )
        )
        copies[-1].start()
    for part in range(PARTS):
        copies[part].wait()
        for block in range(part * share // LX, (part + 1) * share // LX):
            row = block * LX
            for lane in range(0, modes, 128):
                real, imag = [
                    [buffer_ref[r, b, row : row + LX, lane : lane + 128] for b in range(3)]
                    for r in range(2)
                ]

                def weight(a, b, r):
                    return wide_ref[(a * 3 + b) * 2 + r, row : row + LX, :]

                for a in range(3):
                    for r, value in enumerate(color_sum(weight, real, imag, a)):
                        start = right_row(block, r, a, share)
                        right_ref[start : start + LX, lane : lane + 128] = value
        value = jnp.dot(
            left_ref[:, part * width : (part + 1) * width],
            right_ref[part * width : (part + 1) * width, :],
            preferred_element_type=jnp.float32,
        )
        if part:
            value = total_ref[...] + value
        if part == PARTS - 1:
            value = value * scale
        total_ref[...] = value
    store_owned(index_ref, total_ref, outs, 0)


def contract_flat(index, weights, vectors, count, scale):
    _, colors, sites, modes = vectors.shape
    depth = 2 * colors * sites
    out = jax.ShapeDtypeStruct((2, 2 * modes // count, modes), jnp.bfloat16)
    vmem = pl.BlockSpec(memory_space=pltpu.VMEM)
    return pl.pallas_call(
        functools.partial(flat_kernel, scale=scale),
        out_shape=[out] * count
        + [
            pltpu.VMEM((2 * modes, depth), jnp.bfloat16),
            pltpu.VMEM((18, sites, 128), jnp.bfloat16),
        ],
        in_specs=[pl.BlockSpec(memory_space=pltpu.SMEM), vmem, vmem],
        out_specs=[vmem] * (count + 2),
        scratch_shapes=[
            pltpu.VMEM((depth, modes), jnp.bfloat16),
            pltpu.VMEM((2 * modes, modes), jnp.float32),
        ],
        cost_estimate=pl.CostEstimate(
            flops=12 * modes * depth * modes, transcendentals=0, bytes_accessed=4 * depth * modes
        ),
        compiler_params=pltpu.CompilerParams(vmem_limit_bytes=24 << 20),
        name="contract_xy",
    )(index, weights, vectors)


def contract_deep(index, left, wide, source, count, scale):
    _, colors, sites, modes = source.shape
    depth = 2 * colors * sites
    out = jax.ShapeDtypeStruct((1, 2 * modes // count, modes), jnp.bfloat16)
    vmem = pl.BlockSpec(memory_space=pltpu.VMEM)
    return pl.pallas_call(
        functools.partial(deep_kernel, scale=scale),
        out_shape=[out] * count,
        in_specs=[
            pl.BlockSpec(memory_space=pltpu.SMEM),
            vmem,
            vmem,
            pl.BlockSpec(memory_space=pl.ANY),
        ],
        out_specs=[vmem] * count,
        scratch_shapes=[
            pltpu.VMEM(source.shape, jnp.bfloat16),
            pltpu.VMEM((depth, modes), jnp.bfloat16),
            pltpu.VMEM((2 * modes, modes), jnp.float32),
            pltpu.SemaphoreType.DMA((PARTS,)),
        ],
        cost_estimate=pl.CostEstimate(
            flops=4 * modes * depth * modes, transcendentals=0, bytes_accessed=2 * depth * modes
        ),
        compiler_params=pltpu.CompilerParams(vmem_limit_bytes=24 << 20),
        name="contract_z",
    )(
        index,
        in_vmem(left),
        in_vmem(wide),
        source,
    )


def owned_sum(blocks):
    total = blocks[0].astype(jnp.float32)
    for block in blocks[1:]:
        total = total + block.astype(jnp.float32)
    return total.astype(blocks[0].dtype)


def project_kernel(index_ref, factor_ref, *rest, count):
    pieces, (own_ref, out_ref) = rest[:count], rest[-2:]
    size, rows, modes = pieces[0].shape
    even = lax.broadcasted_iota(jnp.int32, (rows, modes), 0) % 2 == 0
    index = index_ref[0]
    for piece, (flip, by) in enumerate(section_order(count)):
        section = (index + by + (1 - 2 * (index % 2)) * flip) % count
        for k in range(size):
            value = pieces[piece][k]
            wide = value.astype(jnp.float32)
            turned = jnp.where(even, -pltpu.roll(wide, rows - 1, 0), pltpu.roll(wide, 1, 0))
            result = jnp.dot(value, factor_ref[0], preferred_element_type=jnp.float32)
            result = result + jnp.dot(
                turned.astype(jnp.bfloat16), factor_ref[1], preferred_element_type=jnp.float32
            )
            out_ref[section, :, k, :, :] = result.astype(jnp.bfloat16).reshape(rows // 2, 2, modes)
            if piece == 0:
                own_ref[:, k, :, :] = value.reshape(rows // 2, 2, modes)


def in_vmem(value):
    return pltpu.with_memory_space_constraint(value, pltpu.VMEM)


def project(index, factor, pieces, total, first, earlier):
    count = len(pieces)
    size, rows, modes = pieces[0].shape
    vmem = pl.BlockSpec(memory_space=pltpu.VMEM)
    kept = pl.BlockSpec(memory_space=pl.ANY)
    step = first // size
    return pl.pallas_call(
        functools.partial(project_kernel, count=count),
        grid=(1,),
        out_shape=[
            jax.ShapeDtypeStruct((rows // 2, total, 2, modes), jnp.bfloat16),
            jax.ShapeDtypeStruct((count, rows // 2, total, 2, modes), jnp.bfloat16),
        ],
        in_specs=[pl.BlockSpec(memory_space=pltpu.SMEM)]
        + [vmem] * (1 + count)
        + [kept] * len(earlier),
        out_specs=[
            pl.BlockSpec((rows // 2, size, 2, modes), lambda i: (0, step, 0, 0)),
            pl.BlockSpec((count, rows // 2, size, 2, modes), lambda i: (0, 0, step, 0, 0)),
        ],
        input_output_aliases={2 + count + i: i for i in range(len(earlier))},
    )(index, *[in_vmem(v) for v in (factor, *pieces)], *earlier)


def exchange(blocks, axis):
    return [blocks[0]] + [shifted_2(blocks[by], axis, by) for by in range(1, len(blocks))]


def paired(axis):
    length = lax.axis_size(axis)
    return [(i, i ^ 1) for i in range(length)]


def section_order(count):
    if count % 2:
        return [(0, by) for by in range(count)]
    return [(flip, by) for flip in range(2) for by in range(0, count, 2)]


def gather(shard, axis, direct):
    length = lax.axis_size(axis)
    stride = 1 if length % 2 else 2
    shards = [shard] + [shifted_2(shard, axis, -by) for by in range(stride, length, stride)]
    if length % 2:
        return shards
    if direct:
        crossed = [
            lax.ppermute(shard, axis, [(((i ^ 1) + by) % length, i) for i in range(length)])
            for by in range(stride, length, stride)
        ]
    partner = [lax.ppermute(shard, axis, paired(axis))]
    if direct:
        return shards + partner + crossed
    return shards + partner + [lax.ppermute(v, axis, paired(axis)) for v in shards[1:]]


def body(eigvecs, links, momenta, perambulators):
    vectors = eigvecs[0]
    _, _, site_count, _ = vectors.shape
    tile_count = lax.axis_size("space")
    tile_index = lax.axis_index("space")
    plane = LX * LY
    forward = shifted_2(vectors[:, :, :plane], "space", -1)
    scale = 1.0 / math.sqrt(6.0 * site_count * tile_count)
    weights = phased_links(links[0], momenta, tile_index, tile_count)
    tile = tile_index.astype(jnp.int32).reshape(1)
    section = lax.axis_index("tm").astype(jnp.int32).reshape(1)
    *flat, left, wide = contract_flat(tile, weights, vectors, tile_count, scale)
    raised = jnp.concatenate([vectors[:, :, plane:], forward], 2)
    flat_parts = exchange(flat, "space")
    deep = contract_deep(tile, left, wide, raised, tile_count, scale)
    flat_parts, _ = lax.optimization_barrier((flat_parts, deep))
    deep_parts = exchange(deep, "space")
    factor = perambulators[0]
    flat_sum = owned_sum(flat_parts)
    flat_pieces = gather(flat_sum, "tm", False)
    earlier = project(section, factor, flat_pieces, 3, 0, ())
    deep_sum = owned_sum(deep_parts)
    deep_pieces = gather(deep_sum, "tm", True)
    own, projected = project(section, factor, deep_pieces, 3, 2, earlier)
    return (own[None], projected[None])


def solution(mesh):
    in_specs = (
        P(("ens", "tm"), None, None, "space", None),
        P(("ens", "tm"), None, None, None, None, "space"),
        P(),
        P(("ens", "tm"), None, None, None),
    )
    out_specs = (
        P(("ens", "tm"), "space", None, None, None),
        P(("ens", "tm"), None, "space", None, None, None),
    )
    return jax.shard_map(body, mesh=mesh, in_specs=in_specs, out_specs=out_specs, check_vma=False)
```

```python
import functools
import math

import jax
import jax.numpy as jnp
from jax import lax
from jax.experimental import pallas as pl
from jax.experimental.pallas import tpu as pltpu
from jax.sharding import PartitionSpec as P

LX = 32
LY = 16
PARTS = 4


def shifted_2(shard, axis, by):
    length = lax.axis_size(axis)
    return lax.ppermute(shard, axis, [(i, (i + by) % length) for i in range(length)])


def phase_angle(momentum, first_pos, second_pos, third_pos, depth):
    weights = momentum.astype(jnp.float32)
    return (
        2.0
        * math.pi
        * (
            weights[0] * first_pos / LX
            + weights[1] * second_pos / LY
            + weights[2] * third_pos / depth
        )
    )


def phased_links(links, momenta, tile_index, tile_count):
    site_count = links.shape[-1]
    planes = site_count // (LX * LY)
    site_index = jnp.arange(site_count, dtype=jnp.int32)
    first_pos = (site_index % LX).astype(jnp.float32)
    second_pos = (site_index // LX % LY).astype(jnp.float32)
    third_pos = (tile_index * planes + site_index // (LX * LY)).astype(jnp.float32)
    angle = jnp.stack(
        [phase_angle(momenta[k], first_pos, second_pos, third_pos, planes * tile_count) for k in range(3)]
    )
    cosine = jnp.cos(angle)[:, None, None]
    sine = jnp.sin(angle)[:, None, None]
    link = links.astype(jnp.float32)
    real = cosine * link[:, 0] + sine * link[:, 1]
    imag = cosine * link[:, 1] - sine * link[:, 0]
    return jnp.stack([real, imag], 3).reshape(3 * 18, site_count).T


def left_rows(source_ref, left_ref):
    _, colors, sites, modes = source_ref.shape
    share = sites // PARTS
    shape = (2 * modes, 2 * modes)
    row = lax.broadcasted_iota(jnp.int32, shape, 0)
    column = lax.broadcasted_iota(jnp.int32, shape, 1)
    one = jnp.ones(shape, jnp.float32)
    zero = jnp.zeros(shape, jnp.float32)
    first = jnp.where(row == 2 * column, one, zero)
    first = first - jnp.where(row == 2 * (column - modes) + 1, one, zero)
    second = jnp.where(row == 2 * column + 1, one, zero)
    second = second + jnp.where(row == 2 * (column - modes), one, zero)
    picks = (first.astype(jnp.bfloat16), second.astype(jnp.bfloat16))
    width = colors * share
    for part in range(PARTS):
        pair = jnp.concatenate(
            [
                source_ref[r, :, part * share : (part + 1) * share, :].reshape(width, modes)
                for r in range(2)
            ],
            1,
        )
        for r in range(2):
            turned = lax.dot_general(
                picks[r], pair, (((1,), (1,)), ((), ())), preferred_element_type=jnp.float32
            )
            start = (part * 2 + r) * width
            left_ref[:, start : start + width] = turned.astype(jnp.bfloat16)


def right_row(block, r, a, share):
    part = block // (share // LX)
    return ((part * 2 + r) * 3 + a - part) * share + block * LX


def color_sum(weight, real, imag, a):
    real_sum = None
    imag_sum = None
    for b in range(3):
        w_real, w_imag = weight(a, b, 0), weight(a, b, 1)
        term_real = w_real * real[b] - w_imag * imag[b]
        term_imag = w_real * imag[b] + w_imag * real[b]
        real_sum = term_real if b == 0 else real_sum + term_real
        imag_sum = term_imag if b == 0 else imag_sum + term_imag
    return real_sum, imag_sum


def store_owned(index_ref, total_ref, outs, slot):
    count = len(outs)
    rows = total_ref.shape[0] // count
    for d in range(count):
        owner = (index_ref[0] + d) % count
        block = total_ref[pl.ds(pl.multiple_of(owner * rows, rows), rows), :]
        outs[d][slot] = block.astype(jnp.bfloat16)


def flat_kernel(index_ref, weights_ref, source_ref, *rest, scale):
    outs, left_ref, wide_ref, right_ref, total_ref = rest[:-4], *rest[-4:]
    sites = source_ref.shape[2]
    share = sites // PARTS
    left_rows(source_ref, left_ref)
    for direction in range(2):

        def step(block, _):
            row = pl.multiple_of(block * LX, LX)
            from_row = row
            if direction == 1:
                plane = block // LY * LY
                from_row = pl.multiple_of((plane + (block - plane + 1) % LY) * LX, LX)
            parts = [
                [source_ref[r, b, pl.ds(from_row, LX), :].astype(jnp.float32) for b in range(3)]
                for r in range(2)
            ]
            if direction == 0:
                parts = [[pltpu.roll(v, LX - 1, 0) for v in part] for part in parts]
            weights = weights_ref[pl.ds(row, LX), :]

            def weight(a, b, r, k=direction):
                column = ((k * 3 + a) * 3 + b) * 2 + r
                return weights[:, column : column + 1]

            for a in range(3):
                for r, value in enumerate(color_sum(weight, *parts, a)):
                    start = pl.multiple_of(right_row(block, r, a, share), LX)
                    right_ref[pl.ds(start, LX), :] = value.astype(jnp.bfloat16)
            if direction == 0:
                for column in range(18):
                    value = weight(0, 0, column, 2).astype(jnp.bfloat16)
                    wide_ref[column, pl.ds(row, LX), :] = jnp.broadcast_to(value, (LX, 128))
            return 0

        lax.fori_loop(0, sites // LX, step, 0)
        total_ref[...] = (
            jnp.dot(left_ref[...], right_ref[...], preferred_element_type=jnp.float32) * scale
        )
        store_owned(index_ref, total_ref, outs, direction)


def deep_kernel(index_ref, left_ref, wide_ref, source_ref, *rest, scale):
    outs, buffer_ref, right_ref, total_ref, sems = rest[:-4], *rest[-4:]
    sites = source_ref.shape[2]
    share = sites // PARTS
    width = left_ref.shape[1] // PARTS
    modes = source_ref.shape[3]
    copies = []
    for part in range(PARTS):
        rows = pl.ds(part * share, share)
        copies.append(
            pltpu.make_async_copy(
                source_ref.at[:, :, rows, :], buffer_ref.at[:, :, rows, :], sems.at[part]
            )
        )
        copies[-1].start()
    for part in range(PARTS):
        copies[part].wait()
        for block in range(part * share // LX, (part + 1) * share // LX):
            row = block * LX
            for lane in range(0, modes, 128):
                real, imag = [
                    [buffer_ref[r, b, row : row + LX, lane : lane + 128] for b in range(3)]
                    for r in range(2)
                ]

                def weight(a, b, r):
                    return wide_ref[(a * 3 + b) * 2 + r, row : row + LX, :]

                for a in range(3):
                    for r, value in enumerate(color_sum(weight, real, imag, a)):
                        start = right_row(block, r, a, share)
                        right_ref[start : start + LX, lane : lane + 128] = value
        value = jnp.dot(
            left_ref[:, part * width : (part + 1) * width],
            right_ref[part * width : (part + 1) * width, :],
            preferred_element_type=jnp.float32,
        )
        if part:
            value = total_ref[...] + value
        if part == PARTS - 1:
            value = value * scale
        total_ref[...] = value
    store_owned(index_ref, total_ref, outs, 0)


def contract_flat(index, weights, vectors, count, scale):
    _, colors, sites, modes = vectors.shape
    depth = 2 * colors * sites
    out = jax.ShapeDtypeStruct((2, 2 * modes // count, modes), jnp.bfloat16)
    vmem = pl.BlockSpec(memory_space=pltpu.VMEM)
    return pl.pallas_call(
        functools.partial(flat_kernel, scale=scale),
        out_shape=[out] * count
        + [
            pltpu.VMEM((2 * modes, depth), jnp.bfloat16),
            pltpu.VMEM((18, sites, 128), jnp.bfloat16),
        ],
        in_specs=[pl.BlockSpec(memory_space=pltpu.SMEM), vmem, vmem],
        out_specs=[vmem] * (count + 2),
        scratch_shapes=[
            pltpu.VMEM((depth, modes), jnp.bfloat16),
            pltpu.VMEM((2 * modes, modes), jnp.float32),
        ],
        cost_estimate=pl.CostEstimate(
            flops=12 * modes * depth * modes, transcendentals=0, bytes_accessed=4 * depth * modes
        ),
        compiler_params=pltpu.CompilerParams(vmem_limit_bytes=24 << 20),
        name="contract_xy",
    )(index, weights, vectors)


def contract_deep(index, left, wide, source, count, scale):
    _, colors, sites, modes = source.shape
    depth = 2 * colors * sites
    out = jax.ShapeDtypeStruct((1, 2 * modes // count, modes), jnp.bfloat16)
    vmem = pl.BlockSpec(memory_space=pltpu.VMEM)
    return pl.pallas_call(
        functools.partial(deep_kernel, scale=scale),
        out_shape=[out] * count,
        in_specs=[
            pl.BlockSpec(memory_space=pltpu.SMEM),
            vmem,
            vmem,
            pl.BlockSpec(memory_space=pl.ANY),
        ],
        out_specs=[vmem] * count,
        scratch_shapes=[
            pltpu.VMEM(source.shape, jnp.bfloat16),
            pltpu.VMEM((depth, modes), jnp.bfloat16),
            pltpu.VMEM((2 * modes, modes), jnp.float32),
            pltpu.SemaphoreType.DMA((PARTS,)),
        ],
        cost_estimate=pl.CostEstimate(
            flops=4 * modes * depth * modes, transcendentals=0, bytes_accessed=2 * depth * modes
        ),
        compiler_params=pltpu.CompilerParams(vmem_limit_bytes=24 << 20),
        name="contract_z",
    )(
        index,
        in_vmem(left),
        in_vmem(wide),
        source,
    )


def owned_sum(blocks):
    total = blocks[0].astype(jnp.float32)
    for block in blocks[1:]:
        total = total + block.astype(jnp.float32)
    return total.astype(blocks[0].dtype)


def in_vmem(value):
    return pltpu.with_memory_space_constraint(value, pltpu.VMEM)


def project_kernel(index_ref, factor_ref, *rest, plan, count, aliased):
    items = len(plan)
    pieces, rest = rest[:items], rest[items + aliased :]
    own_ref, out_ref, sems = rest[0], rest[1], rest[-1]
    buffers = list(rest[2:-1])
    index = index_ref[0]
    copies = []
    for slot, (flip, by, first) in enumerate(plan):
        piece_ref, buffer_ref = pieces[slot], buffers[slot]
        size, rows, modes = piece_ref.shape
        section = (index + by + (1 - 2 * (index % 2)) * flip) % count
        even = lax.broadcasted_iota(jnp.int32, (rows, modes), 0) % 2 == 0
        for k in range(size):
            value = piece_ref[k]
            wide = value.astype(jnp.float32)
            turned = jnp.where(even, -pltpu.roll(wide, rows - 1, 0), pltpu.roll(wide, 1, 0))
            result = jnp.dot(value, factor_ref[0], preferred_element_type=jnp.float32)
            result = result + jnp.dot(
                turned.astype(jnp.bfloat16), factor_ref[1], preferred_element_type=jnp.float32
            )
            buffer_ref[:, k, :, :] = result.astype(jnp.bfloat16).reshape(rows // 2, 2, modes)
        momenta = pl.ds(first, size)
        copies.append(
            pltpu.make_async_copy(buffer_ref, out_ref.at[section, :, momenta], sems.at[len(copies)])
        )
        copies[-1].start()
        if flip == 0 and by == 0:
            kept_ref = buffers[-1]
            for k in range(size):
                kept_ref[:, k, :, :] = piece_ref[k].reshape(rows // 2, 2, modes)
            copies.append(
                pltpu.make_async_copy(kept_ref, own_ref.at[:, momenta], sems.at[len(copies)])
            )
            copies[-1].start()
    for copy in copies:
        copy.wait()


def project(index, factor, plan, pieces, total, count, earlier):
    _, rows, modes = pieces[0].shape
    vmem = pl.BlockSpec(memory_space=pltpu.VMEM)
    kept = pl.BlockSpec(memory_space=pl.ANY)
    own = [piece for piece, entry in zip(pieces, plan) if entry[:2] == (0, 0)]
    buffers = [
        pltpu.VMEM((rows // 2, piece.shape[0], 2, modes), jnp.bfloat16)
        for piece in list(pieces) + own
    ]
    return pl.pallas_call(
        functools.partial(project_kernel, plan=plan, count=count, aliased=len(earlier)),
        out_shape=[
            jax.ShapeDtypeStruct((rows // 2, total, 2, modes), jnp.bfloat16),
            jax.ShapeDtypeStruct((count, rows // 2, total, 2, modes), jnp.bfloat16),
        ],
        in_specs=[pl.BlockSpec(memory_space=pltpu.SMEM)]
        + [vmem] * (1 + len(pieces))
        + [kept] * len(earlier),
        out_specs=[kept, kept],
        scratch_shapes=buffers + [pltpu.SemaphoreType.DMA((len(pieces) + len(own),))],
        input_output_aliases={2 + len(pieces) + i: i for i in range(len(earlier))},
        compiler_params=pltpu.CompilerParams(vmem_limit_bytes=24 << 20),
    )(index, *[in_vmem(v) for v in (factor, *pieces)], *earlier)


def exchange(blocks, axis):
    length = len(blocks)
    steps = sorted(range(1, length), key=lambda by: (min(by, length - by) == 1, by))
    return [blocks[0]] + [shifted_2(blocks[by], axis, by) for by in steps]


def paired(axis):
    length = lax.axis_size(axis)
    return [(i, i ^ 1) for i in range(length)]


def section_order(count):
    if count % 2:
        return [(0, by) for by in range(count)]
    return [(flip, by) for flip in range(2) for by in range(0, count, 2)]


def gather(shard, axis, direct):
    length = lax.axis_size(axis)
    stride = 1 if length % 2 else 2
    shards = [shard] + [shifted_2(shard, axis, -by) for by in range(stride, length, stride)]
    if length % 2:
        return shards
    if direct:
        crossed = [
            lax.ppermute(shard, axis, [(((i ^ 1) + by) % length, i) for i in range(length)])
            for by in range(stride, length, stride)
        ]
    partner = [lax.ppermute(shard, axis, paired(axis))]
    if direct:
        return shards + partner + crossed
    return shards + partner + [lax.ppermute(v, axis, paired(axis)) for v in shards[1:]]


def body(eigvecs, links, momenta, perambulators):
    vectors = eigvecs[0]
    _, _, site_count, _ = vectors.shape
    tile_count = lax.axis_size("space")
    tile_index = lax.axis_index("space")
    plane = LX * LY
    forward = shifted_2(vectors[:, :, :plane], "space", -1)
    scale = 1.0 / math.sqrt(6.0 * site_count * tile_count)
    weights = phased_links(links[0], momenta, tile_index, tile_count)
    tile = tile_index.astype(jnp.int32).reshape(1)
    section = lax.axis_index("tm").astype(jnp.int32).reshape(1)
    *flat, left, wide = contract_flat(tile, weights, vectors, tile_count, scale)
    raised = jnp.concatenate([vectors[:, :, plane:], forward], 2)
    flat_parts = exchange(flat, "space")
    deep = contract_deep(tile, left, wide, raised, tile_count, scale)
    flat_parts, _ = lax.optimization_barrier((flat_parts, deep))
    deep_parts = exchange(deep, "space")
    factor = perambulators[0]
    flat_sum = owned_sum(flat_parts)
    flat_pieces = gather(flat_sum, "tm", False)
    section_count = lax.axis_size("tm")
    order = section_order(section_count)
    flat_plan = tuple((flip, by, 0) for flip, by in order)
    deep_plan = tuple((flip, by, 2) for flip, by in order)
    early = section_count if section_count % 2 else section_count // 2 + 1
    earlier = project(section, factor, flat_plan[:early], flat_pieces[:early], 3, section_count, ())
    deep_sum = owned_sum(deep_parts)
    deep_pieces = gather(deep_sum, "tm", True)
    own, projected = project(
        section,
        factor,
        flat_plan[early:] + deep_plan,
        flat_pieces[early:] + deep_pieces,
        3,
        section_count,
        earlier,
    )
    return (own[None], projected[None])


def solution(mesh):
    in_specs = (
        P(("ens", "tm"), None, None, "space", None),
        P(("ens", "tm"), None, None, None, None, "space"),
        P(),
        P(("ens", "tm"), None, None, None),
    )
    out_specs = (
        P(("ens", "tm"), "space", None, None, None),
        P(("ens", "tm"), None, "space", None, None, None),
    )
    return jax.shard_map(body, mesh=mesh, in_specs=in_specs, out_specs=out_specs, check_vma=False)
```

```python
import functools
import math

import jax
import jax.numpy as jnp
from jax import lax
from jax.experimental import pallas as pl
from jax.experimental.pallas import tpu as pltpu
from jax.sharding import PartitionSpec as P

LX = 32
LY = 16
PARTS = 4


def shifted_2(shard, axis, by):
    length = lax.axis_size(axis)
    return lax.ppermute(shard, axis, [(i, (i + by) % length) for i in range(length)])


def phase_angle(momentum, first_pos, second_pos, third_pos, depth):
    weights = momentum.astype(jnp.float32)
    return (
        2.0
        * math.pi
        * (
            weights[0] * first_pos / LX
            + weights[1] * second_pos / LY
            + weights[2] * third_pos / depth
        )
    )


def phased_links(links, momenta, tile_index, tile_count):
    site_count = links.shape[-1]
    planes = site_count // (LX * LY)
    site_index = jnp.arange(site_count, dtype=jnp.int32)
    first_pos = (site_index % LX).astype(jnp.float32)
    second_pos = (site_index // LX % LY).astype(jnp.float32)
    third_pos = (tile_index * planes + site_index // (LX * LY)).astype(jnp.float32)
    angle = jnp.stack(
        [phase_angle(momenta[k], first_pos, second_pos, third_pos, planes * tile_count) for k in range(3)]
    )
    cosine = jnp.cos(angle)[:, None, None]
    sine = jnp.sin(angle)[:, None, None]
    link = links.astype(jnp.float32)
    real = cosine * link[:, 0] + sine * link[:, 1]
    imag = cosine * link[:, 1] - sine * link[:, 0]
    return jnp.stack([real, imag], 3).reshape(3 * 18, site_count).T


def left_rows(source_ref, left_ref):
    _, colors, sites, modes = source_ref.shape
    share = sites // PARTS
    shape = (2 * modes, 2 * modes)
    row = lax.broadcasted_iota(jnp.int32, shape, 0)
    column = lax.broadcasted_iota(jnp.int32, shape, 1)
    one = jnp.ones(shape, jnp.float32)
    zero = jnp.zeros(shape, jnp.float32)
    first = jnp.where(row == 2 * column, one, zero)
    first = first - jnp.where(row == 2 * (column - modes) + 1, one, zero)
    second = jnp.where(row == 2 * column + 1, one, zero)
    second = second + jnp.where(row == 2 * (column - modes), one, zero)
    picks = (first.astype(jnp.bfloat16), second.astype(jnp.bfloat16))
    width = colors * share
    for part in range(PARTS):
        pair = jnp.concatenate(
            [
                source_ref[r, :, part * share : (part + 1) * share, :].reshape(width, modes)
                for r in range(2)
            ],
            1,
        )
        for r in range(2):
            turned = lax.dot_general(
                picks[r], pair, (((1,), (1,)), ((), ())), preferred_element_type=jnp.float32
            )
            start = (part * 2 + r) * width
            left_ref[:, start : start + width] = turned.astype(jnp.bfloat16)


def right_row(block, r, a, share):
    part = block // (share // LX)
    return ((part * 2 + r) * 3 + a - part) * share + block * LX


def color_sum(weight, real, imag, a):
    real_sum = None
    imag_sum = None
    for b in range(3):
        w_real, w_imag = weight(a, b, 0), weight(a, b, 1)
        term_real = w_real * real[b] - w_imag * imag[b]
        term_imag = w_real * imag[b] + w_imag * real[b]
        real_sum = term_real if b == 0 else real_sum + term_real
        imag_sum = term_imag if b == 0 else imag_sum + term_imag
    return real_sum, imag_sum


def store_owned(index_ref, total_ref, outs, slot):
    count = len(outs)
    rows = total_ref.shape[0] // count
    for d in range(count):
        owner = (index_ref[0] + d) % count
        block = total_ref[pl.ds(pl.multiple_of(owner * rows, rows), rows), :]
        outs[d][slot] = block.astype(jnp.bfloat16)


def flat_kernel(index_ref, weights_ref, source_ref, *rest, scale):
    outs, left_ref, wide_ref, right_ref, total_ref = rest[:-4], *rest[-4:]
    sites = source_ref.shape[2]
    share = sites // PARTS
    left_rows(source_ref, left_ref)
    for direction in range(2):

        def step(block, _):
            row = pl.multiple_of(block * LX, LX)
            from_row = row
            if direction == 1:
                plane = block // LY * LY
                from_row = pl.multiple_of((plane + (block - plane + 1) % LY) * LX, LX)
            parts = [
                [source_ref[r, b, pl.ds(from_row, LX), :].astype(jnp.float32) for b in range(3)]
                for r in range(2)
            ]
            if direction == 0:
                parts = [[pltpu.roll(v, LX - 1, 0) for v in part] for part in parts]
            weights = weights_ref[pl.ds(row, LX), :]

            def weight(a, b, r, k=direction):
                column = ((k * 3 + a) * 3 + b) * 2 + r
                return weights[:, column : column + 1]

            for a in range(3):
                for r, value in enumerate(color_sum(weight, *parts, a)):
                    start = pl.multiple_of(right_row(block, r, a, share), LX)
                    right_ref[pl.ds(start, LX), :] = value.astype(jnp.bfloat16)
            if direction == 0:
                for column in range(18):
                    value = weight(0, 0, column, 2).astype(jnp.bfloat16)
                    wide_ref[column, pl.ds(row, LX), :] = jnp.broadcast_to(value, (LX, 128))
            return 0

        lax.fori_loop(0, sites // LX, step, 0)
        total_ref[...] = (
            jnp.dot(left_ref[...], right_ref[...], preferred_element_type=jnp.float32) * scale
        )
        store_owned(index_ref, total_ref, outs, direction)


def deep_kernel(index_ref, left_ref, wide_ref, source_ref, *rest, scale):
    outs, buffer_ref, right_ref, total_ref, sems = rest[:-4], *rest[-4:]
    sites = source_ref.shape[2]
    share = sites // PARTS
    width = left_ref.shape[1] // PARTS
    modes = source_ref.shape[3]
    copies = []
    for part in range(PARTS):
        rows = pl.ds(part * share, share)
        copies.append(
            pltpu.make_async_copy(
                source_ref.at[:, :, rows, :], buffer_ref.at[:, :, rows, :], sems.at[part]
            )
        )
        copies[-1].start()
    for part in range(PARTS):
        copies[part].wait()
        for block in range(part * share // LX, (part + 1) * share // LX):
            row = block * LX
            for lane in range(0, modes, 128):
                real, imag = [
                    [buffer_ref[r, b, row : row + LX, lane : lane + 128] for b in range(3)]
                    for r in range(2)
                ]

                def weight(a, b, r):
                    return wide_ref[(a * 3 + b) * 2 + r, row : row + LX, :]

                for a in range(3):
                    for r, value in enumerate(color_sum(weight, real, imag, a)):
                        start = right_row(block, r, a, share)
                        right_ref[start : start + LX, lane : lane + 128] = value
        value = jnp.dot(
            left_ref[:, part * width : (part + 1) * width],
            right_ref[part * width : (part + 1) * width, :],
            preferred_element_type=jnp.float32,
        )
        if part:
            value = total_ref[...] + value
        if part == PARTS - 1:
            value = value * scale
        total_ref[...] = value
    store_owned(index_ref, total_ref, outs, 0)


def contract_flat(index, weights, vectors, count, scale):
    _, colors, sites, modes = vectors.shape
    depth = 2 * colors * sites
    out = jax.ShapeDtypeStruct((2, 2 * modes // count, modes), jnp.bfloat16)
    vmem = pl.BlockSpec(memory_space=pltpu.VMEM)
    return pl.pallas_call(
        functools.partial(flat_kernel, scale=scale),
        out_shape=[out] * count
        + [
            pltpu.VMEM((2 * modes, depth), jnp.bfloat16),
            pltpu.VMEM((18, sites, 128), jnp.bfloat16),
        ],
        in_specs=[pl.BlockSpec(memory_space=pltpu.SMEM), vmem, vmem],
        out_specs=[vmem] * (count + 2),
        scratch_shapes=[
            pltpu.VMEM((depth, modes), jnp.bfloat16),
            pltpu.VMEM((2 * modes, modes), jnp.float32),
        ],
        cost_estimate=pl.CostEstimate(
            flops=12 * modes * depth * modes, transcendentals=0, bytes_accessed=4 * depth * modes
        ),
        compiler_params=pltpu.CompilerParams(vmem_limit_bytes=24 << 20),
        name="contract_xy",
    )(index, weights, vectors)


def contract_deep(index, left, wide, source, count, scale):
    _, colors, sites, modes = source.shape
    depth = 2 * colors * sites
    out = jax.ShapeDtypeStruct((1, 2 * modes // count, modes), jnp.bfloat16)
    vmem = pl.BlockSpec(memory_space=pltpu.VMEM)
    return pl.pallas_call(
        functools.partial(deep_kernel, scale=scale),
        out_shape=[out] * count,
        in_specs=[
            pl.BlockSpec(memory_space=pltpu.SMEM),
            vmem,
            vmem,
            pl.BlockSpec(memory_space=pl.ANY),
        ],
        out_specs=[vmem] * count,
        scratch_shapes=[
            pltpu.VMEM(source.shape, jnp.bfloat16),
            pltpu.VMEM((depth, modes), jnp.bfloat16),
            pltpu.VMEM((2 * modes, modes), jnp.float32),
            pltpu.SemaphoreType.DMA((PARTS,)),
        ],
        cost_estimate=pl.CostEstimate(
            flops=4 * modes * depth * modes, transcendentals=0, bytes_accessed=2 * depth * modes
        ),
        compiler_params=pltpu.CompilerParams(vmem_limit_bytes=24 << 20),
        name="contract_z",
    )(
        index,
        in_vmem(left),
        in_vmem(wide),
        source,
    )


def owned_sum(blocks):
    total = blocks[0].astype(jnp.float32)
    for block in blocks[1:]:
        total = total + block.astype(jnp.float32)
    return total.astype(blocks[0].dtype)


def in_vmem(value):
    return pltpu.with_memory_space_constraint(value, pltpu.VMEM)


def project_kernel(index_ref, factor_ref, *rest, plan, count, aliased):
    items = len(plan)
    pieces, rest = rest[:items], rest[items + aliased :]
    own_ref, out_ref, sems = rest[0], rest[1], rest[-1]
    buffers = list(rest[2:-1])
    index = index_ref[0]
    copies = []
    for slot, (flip, by, first) in enumerate(plan):
        piece_ref, buffer_ref = pieces[slot], buffers[slot]
        size, rows, modes = piece_ref.shape
        section = (index + by + (1 - 2 * (index % 2)) * flip) % count
        even = lax.broadcasted_iota(jnp.int32, (rows, modes), 0) % 2 == 0
        for k in range(size):
            value = piece_ref[k]
            wide = value.astype(jnp.float32)
            turned = jnp.where(even, -pltpu.roll(wide, rows - 1, 0), pltpu.roll(wide, 1, 0))
            result = jnp.dot(value, factor_ref[0], preferred_element_type=jnp.float32)
            result = result + jnp.dot(
                turned.astype(jnp.bfloat16), factor_ref[1], preferred_element_type=jnp.float32
            )
            buffer_ref[:, k, :, :] = result.astype(jnp.bfloat16).reshape(rows // 2, 2, modes)
        momenta = pl.ds(first, size)
        copies.append(
            pltpu.make_async_copy(buffer_ref, out_ref.at[section, :, momenta], sems.at[len(copies)])
        )
        copies[-1].start()
        if flip == 0 and by == 0:
            kept_ref = buffers[-1]
            for k in range(size):
                kept_ref[:, k, :, :] = piece_ref[k].reshape(rows // 2, 2, modes)
            copies.append(
                pltpu.make_async_copy(kept_ref, own_ref.at[:, momenta], sems.at[len(copies)])
            )
            copies[-1].start()
    for copy in copies:
        copy.wait()


def project(index, factor, plan, pieces, total, count, earlier):
    _, rows, modes = pieces[0].shape
    vmem = pl.BlockSpec(memory_space=pltpu.VMEM)
    kept = pl.BlockSpec(memory_space=pl.ANY)
    own = [piece for piece, entry in zip(pieces, plan) if entry[:2] == (0, 0)]
    buffers = [
        pltpu.VMEM((rows // 2, piece.shape[0], 2, modes), jnp.bfloat16)
        for piece in list(pieces) + own
    ]
    return pl.pallas_call(
        functools.partial(project_kernel, plan=plan, count=count, aliased=len(earlier)),
        out_shape=[
            jax.ShapeDtypeStruct((rows // 2, total, 2, modes), jnp.bfloat16),
            jax.ShapeDtypeStruct((count, rows // 2, total, 2, modes), jnp.bfloat16),
        ],
        in_specs=[pl.BlockSpec(memory_space=pltpu.SMEM)]
        + [vmem] * (1 + len(pieces))
        + [kept] * len(earlier),
        out_specs=[kept, kept],
        scratch_shapes=buffers + [pltpu.SemaphoreType.DMA((len(pieces) + len(own),))],
        input_output_aliases={2 + len(pieces) + i: i for i in range(len(earlier))},
        compiler_params=pltpu.CompilerParams(vmem_limit_bytes=24 << 20),
    )(index, *[in_vmem(v) for v in (factor, *pieces)], *earlier)


def exchange(blocks, axis, far_last):
    length = len(blocks)
    steps = range(1, length)
    if far_last:
        steps = sorted(steps, key=lambda by: (min(by, length - by) == 1, by))
    return [blocks[0]] + [shifted_2(blocks[by], axis, by) for by in steps]


def paired(axis):
    length = lax.axis_size(axis)
    return [(i, i ^ 1) for i in range(length)]


def section_order(count):
    if count % 2:
        return [(0, by) for by in range(count)]
    return [(flip, by) for flip in range(2) for by in range(0, count, 2)]


def gather(shard, axis, direct):
    length = lax.axis_size(axis)
    stride = 1 if length % 2 else 2
    shards = [shard] + [shifted_2(shard, axis, -by) for by in range(stride, length, stride)]
    if length % 2:
        return shards
    if direct:
        crossed = [
            lax.ppermute(shard, axis, [(((i ^ 1) + by) % length, i) for i in range(length)])
            for by in range(stride, length, stride)
        ]
    partner = [lax.ppermute(shard, axis, paired(axis))]
    if direct:
        return shards + partner + crossed
    return shards + partner + [lax.ppermute(v, axis, paired(axis)) for v in shards[1:]]


def body(eigvecs, links, momenta, perambulators):
    vectors = eigvecs[0]
    _, _, site_count, _ = vectors.shape
    tile_count = lax.axis_size("space")
    tile_index = lax.axis_index("space")
    plane = LX * LY
    forward = shifted_2(vectors[:, :, :plane], "space", -1)
    scale = 1.0 / math.sqrt(6.0 * site_count * tile_count)
    weights = phased_links(links[0], momenta, tile_index, tile_count)
    tile = tile_index.astype(jnp.int32).reshape(1)
    section = lax.axis_index("tm").astype(jnp.int32).reshape(1)
    *flat, left, wide = contract_flat(tile, weights, vectors, tile_count, scale)
    raised = jnp.concatenate([vectors[:, :, plane:], forward], 2)
    flat_parts = exchange(flat, "space", True)
    deep = contract_deep(tile, left, wide, raised, tile_count, scale)
    flat_parts, _ = lax.optimization_barrier((flat_parts, deep))
    deep_parts = exchange(deep, "space", False)
    factor = perambulators[0]
    flat_sum = owned_sum(flat_parts)
    flat_pieces = gather(flat_sum, "tm", False)
    section_count = lax.axis_size("tm")
    order = section_order(section_count)
    flat_plan = tuple((flip, by, 0) for flip, by in order)
    deep_plan = tuple((flip, by, 2) for flip, by in order)
    early = section_count if section_count % 2 else section_count // 2 + 1
    earlier = project(section, factor, flat_plan[:early], flat_pieces[:early], 3, section_count, ())
    deep_sum = owned_sum(deep_parts)
    deep_pieces = gather(deep_sum, "tm", True)
    own, projected = project(
        section,
        factor,
        flat_plan[early:] + deep_plan,
        flat_pieces[early:] + deep_pieces,
        3,
        section_count,
        earlier,
    )
    return (own[None], projected[None])


def solution(mesh):
    in_specs = (
        P(("ens", "tm"), None, None, "space", None),
        P(("ens", "tm"), None, None, None, None, "space"),
        P(),
        P(("ens", "tm"), None, None, None),
    )
    out_specs = (
        P(("ens", "tm"), "space", None, None, None),
        P(("ens", "tm"), None, "space", None, None, None),
    )
    return jax.shard_map(body, mesh=mesh, in_specs=in_specs, out_specs=out_specs, check_vma=False)
```
